128 devices in a mesh: tm: 128 (over z, x, y, core).
Axes of the slice: x: 4, y: 4, z: 4, core: 2. Of those that a mesh axis runs over, the one named last changes fastest.
Arguments:
- measurements: float32 [1024, 192, 512], P('tm'), may hold values from -8 to 8
- observed: int32 [1024], P('tm'), may hold values 0 or 1
- segment_ids: int32 [1024], P('tm'), may hold values from 0 to 31, never falling along the last dimension, each value on 1 to 64 neighbouring positions
- courant_table: float32 [32, 4], replicated, may hold values from 0.15 to 0.6
- filter_gains: float32 [192], replicated, may hold values from 0.0005 to 0.08
- initial_state: float32 [192, 512], replicated, may hold values from -6 to 6
Outputs:
- filtered: float32 [1024, 192, 512], P('tm')
- consistency: float32 [512], replicated
The draws below stay inside these ranges and needn't reach their ends.
Inputs may be any that keep to these rules, and one draw needn't show every extreme that they name: `segment_ids`: the segment number never falls along time; each segment lasts 1 to 64 steps, one exactly that.
All inputs are finite; a program needn't handle non-finite values. No bound on the sum of `observed` on one device may be relied on, other than what follows from the above.
Results may differ from the reference program's by a relative error of at most 0.0003.
Values sent between devices are 32-bit elements; how exact they have to be, the bound alone decides.
A program may use at most 192 MiB of HBM per device.

```python
import math
import jax
import jax.numpy as jnp
import numpy as np
from jax import lax

CABLES = 4
HALF = 24
STATES = 192
SEGS = 32
FLIGHTS = 512
STEPS = 1024


def draw_filter_gains(key, part):
    key_count = jax.random.fold_in(key, 11)
    key_order = jax.random.fold_in(key, 12)
    key_slow = jax.random.fold_in(key, 13)
    key_fast = jax.random.fold_in(key, 14)
    slow_total = jax.random.randint(key_count, (), 2, CABLES)
    order = jax.random.permutation(key_order, CABLES)
    slow_cable = order < slow_total
    cable_of = jnp.arange(STATES) % (CABLES * HALF) // HALF
    slow_state = jnp.take(slow_cable, cable_of)
    slow_rate = jnp.exp(jax.random.uniform(key_slow, (STATES,), jnp.float32, jnp.log(0.0005), jnp.log(0.002)))
    fast_rate = jnp.exp(jax.random.uniform(key_fast, (STATES,), jnp.float32, jnp.log(0.03), jnp.log(0.08)))
    return jnp.where(slow_state, slow_rate, fast_rate).astype(jnp.float32)


def draw_measurements(key, part):
    times = jnp.arange(STEPS).astype(jnp.float32)[:, None, None] / (STEPS - 1)
    key_main = jax.random.fold_in(key, 21)
    values = jnp.clip(jax.random.normal(key_main, (STEPS, STATES, FLIGHTS), jnp.float32), -5.0, 5.0)
    values = values * (0.5 + times)
    return values.astype(jnp.float32)


def place_ends(array, key, least, largest):
    shape = array.shape
    spot = [jax.random.randint(jax.random.fold_in(key, axis), (), 0, shape[axis]) for axis in range(len(shape))]
    array = array.at[tuple(spot)].set(least)
    longest = shape.index(max(shape))
    spot[longest] = (spot[longest] + 1) % shape[longest]
    return array.at[tuple(spot)].set(largest)


def profile(number_of, total, reach, slope):
    weights = [(1 << 20) // math.isqrt(grade ** slope) + 1 for grade in range(2, number_of + 1)]
    surplus, given = total - reach - (number_of - 1), [1] * (number_of - 1)
    while surplus > 0:
        candidates = [i for i in range(number_of - 1) if given[i] < reach]
        pool, budget = sum([weights[i] for i in candidates]), surplus
        for i in candidates:
            addition = min(reach - given[i], max(1, budget * weights[i] // pool), surplus)
            given[i] = given[i] + addition
            surplus = surplus - addition
    return np.array([reach] + given)


def ragged(stream_key, number_of, total, limit, lean):
    if number_of == 2:
        one = jax.random.randint(stream_key, (), max(1, total - limit), min(limit, total - 1) + 1)
        return jnp.stack([one, total - one])
    lengths = jnp.asarray(profile(number_of, total, limit, lean), jnp.int32)
    couples = (number_of - 1) // 2
    donor, taker = lengths[1:1 + 2 * couples:2], lengths[2:2 + 2 * couples:2]
    room = jnp.minimum(donor - 1, limit - taker)
    moved = jax.random.randint(jax.random.fold_in(stream_key, 1), (couples,), 0, 1 << 20) % (room + 1)
    lengths = lengths.at[1:1 + 2 * couples:2].set(donor - moved).at[2:2 + 2 * couples:2].set(taker + moved)
    return lengths[jax.random.permutation(jax.random.fold_in(stream_key, 2), number_of)]


def normal_values(own_key, shape, spread, most, held_as=jnp.bfloat16):
    values = jax.random.normal(own_key, shape, jnp.float32) * spread
    return jnp.minimum(jnp.maximum(values, -most), most).astype(held_as)


def setup_inputs(seed: int = 0) -> dict:
    streams_of = jax.random.split(jax.random.key(seed), 7)
    return {
        "measurements": draw_measurements(jax.random.fold_in(streams_of[6], 71), 0),
        "observed": place_ends((jax.random.randint(streams_of[1], (STEPS,), 0, 4) < 3).astype(jnp.int32), jax.random.fold_in(streams_of[1], 1), 0, 1),
        "segment_ids": jnp.searchsorted(jnp.cumsum(ragged(streams_of[2], SEGS, STEPS, STEPS // 16, 1)), jnp.arange(STEPS), side="right").astype(jnp.int32),
        "courant_table": jnp.clip(jnp.exp(jax.random.uniform(streams_of[3], (SEGS, CABLES), jnp.float32, math.log(0.15), math.log(0.6))), 0.15, 0.6),
        "filter_gains": draw_filter_gains(jax.random.fold_in(streams_of[6], 71), 0),
        "initial_state": normal_values(streams_of[5], (STATES, FLIGHTS), 1.0, 6.0, jnp.float32),
    }


PAYLOAD = 0.3
HIGHEST = lax.Precision.HIGHEST


def coupling_pattern():
    count = CABLES * HALF
    indices = jnp.arange(count)
    cable_of = indices // HALF
    node_of = indices % HALF
    same = cable_of[:, None] == cable_of[None, :]
    lower = same & (indices[:, None] == indices[None, :] + 1)
    ends = (node_of[:, None] == HALF - 1) & (node_of[None, :] == HALF - 1) & jnp.logical_not(same)
    pattern = jnp.eye(count, dtype=jnp.float32) - lower.astype(jnp.float32) - PAYLOAD * ends.astype(jnp.float32)
    return pattern, cable_of


def transitions_from(courant):
    pattern, cable_of = coupling_pattern()
    member = (cable_of[:, None] == jnp.arange(CABLES)[None, :]).astype(jnp.float32)
    row_scale = jnp.einsum("sc,rc->sr", courant, member, precision=HIGHEST)
    coupled = row_scale[:, :, None] * pattern[None]
    gram = jnp.einsum("sji,sjk->sik", coupled, coupled, precision=HIGHEST)
    ident = jnp.broadcast_to(jnp.eye(pattern.shape[0], dtype=jnp.float32), coupled.shape)
    upper_rows = jnp.concatenate([ident - gram, -jnp.swapaxes(coupled, 1, 2)], axis=2)
    lower_rows = jnp.concatenate([coupled, ident], axis=2)
    return jnp.concatenate([upper_rows, lower_rows], axis=1)


def reference(measurements, observed, segment_ids, courant_table, filter_gains, initial_state):
    def advance(state, inputs):
        segment, flag, sample = inputs
        courant = courant_table[segment][None, :]
        transition = transitions_from(courant)[0]
        predicted = jnp.dot(transition, state, precision=HIGHEST, preferred_element_type=jnp.float32)
        innovation = sample - predicted
        weight = flag.astype(jnp.float32)
        updated = predicted + weight * filter_gains[:, None] * innovation
        power = weight * jnp.sum(innovation * innovation, axis=0)
        return updated, (updated, power)

    last_state, (filtered, powers) = lax.scan(advance, initial_state, (segment_ids, observed, measurements))
    consistency = jnp.sum(powers, axis=0) / (STEPS * STATES)
    return filtered, consistency
```

```python
import functools

import jax
import jax.numpy as jnp
from jax import lax
from jax.experimental import pallas as pl
from jax.experimental.pallas import tpu as pltpu
from jax.sharding import PartitionSpec as P

CABLES = 4
HALF = 24
SIDE = CABLES * HALF
STATES = 2 * SIDE
SEGS = 32
PAYLOAD = 0.3
CORES = 2
MESH = pl.DeviceIdType.MESH
VREGS = SIDE // 8
F32 = jnp.float32


def torus_of(devices):
    return {128: (4, 4, 4), 16: (2, 2, 2)}[devices]


def lanes(tile):
    return pl.ds(pl.multiple_of(tile * 128, 128), 128)


class Rows:
    def __init__(self):
        row = lax.broadcasted_iota(jnp.int32, (8, 128), 0)
        self.first = row == 0
        self.last = row == 7
        self.pay = jnp.where(self.last, F32(PAYLOAD), F32(0.0))
        self.zero = jnp.zeros((8, 128), F32)
        self.low = lax.broadcasted_iota(jnp.int32, (8, 128), 1) < 64


def leap(rows, q, p, w):
    rolled = [pltpu.roll(v, 1, 0) for v in q]
    total = (q[2] + q[5]) + (q[8] + q[11])
    new_p, u = [], []
    for v in range(VREGS):
        before = jnp.where(rows.first, rolled[v - 1] if v % 3 else rows.zero, rolled[v])
        d = q[v] - before
        if v % 3 == 2:
            d = d - rows.pay * (total - q[v])
        new_p.append(p[v] + w[v // 3] * d)
        u.append(w[v // 3] * new_p[v])
    rolled = [pltpu.roll(v, 7, 0) for v in u]
    total = (u[2] + u[5]) + (u[8] + u[11])
    new_q = []
    for v in range(VREGS):
        after = jnp.where(rows.last, rolled[v + 1] if v % 3 < 2 else rows.zero, rolled[v])
        e = u[v] - after
        if v % 3 == 2:
            e = e - rows.pay * (total - u[v])
        new_q.append(q[v] - e)
    return new_q, new_p


def pack(rows, q, p, half):
    if half == 0:
        return [jnp.where(rows.low, a, pltpu.roll(b, 64, 1)) for a, b in zip(q, p)]
    return [jnp.where(rows.low, pltpu.roll(a, 64, 1), b) for a, b in zip(q, p)]


def kernel(
    dims, runs, steps,
    seg_ref, obs_ref, table_ref, gains_ref, m_hbm, x0_hbm,
    out_hbm, power_ref,
    mb, x0b, gain_rows, keep, params_v, params_s, bpack, bin_, maps, prefix, xin, sums, zin, zout,
    start, sout, sin, powers,
    m_sem, out_sem, loc_sem,
    par_s, par_r, up_s, up_r, mx_s, mx_r, mp_s, mp_r, x_s, x_r, z_s, z_r, dn_s, dn_r, pw_s, pw_r,
):
    nz, nx, ny = dims
    ring = ny * CORES
    here = steps
    tiles = runs // 128
    me = lax.axis_index("tm")
    r = lax.rem(me, ring)
    core = lax.rem(me, CORES)
    x = lax.rem(me // ring, nx)
    z = me // (ring * nx)
    base = me - r
    rows = Rows()

    def ring_dev(k):
        return base + lax.rem(r + k, ring)

    def x_dev(k):
        return (z * nx + lax.rem(x + k, nx)) * ring + r

    def z_dev(k):
        return (lax.rem(z + k, nz) * nx + x) * ring + r

    def send(src, dst, ssem, rsem, dev):
        return pltpu.make_async_remote_copy(
            src_ref=src, dst_ref=dst, send_sem=ssem, recv_sem=rsem, device_id=(dev,), device_id_type=MESH
        )

    loads = []
    for f in range(tiles):
        c = pltpu.make_async_copy(m_hbm.at[:, :, pl.ds(f * 128, 128)], mb.at[f], m_sem.at[f])
        c.start()
        loads.append(c)

    barrier = pltpu.get_barrier_semaphore()
    for k in range(1, ring):
        pl.semaphore_signal(barrier, inc=1, device_id=(ring_dev(k),), device_id_type=MESH)
    for k in range(1, nx):
        pl.semaphore_signal(barrier, inc=1, device_id=(x_dev(k),), device_id_type=MESH)
    for k in range(1, nz):
        pl.semaphore_signal(barrier, inc=1, device_id=(z_dev(k),), device_id_type=MESH)

    @pl.when(me == 0)
    def _():
        c = pltpu.make_async_copy(x0_hbm, x0b, loc_sem.at[0])
        c.start()
        c.wait()

    @pl.when(me > 0)
    def _():
        x0b[...] = jnp.zeros_like(x0b)

    row_i = lax.broadcasted_iota(jnp.int32, (8, 128), 0)
    lane_i = lax.broadcasted_iota(jnp.int32, (8, 128), 1)
    tile = jnp.zeros((8, 128), jnp.int32)
    for t in range(here):
        tile = jnp.where((row_i == 0) & (lane_i == t), seg_ref[t], tile)
        tile = jnp.where((row_i == 1) & (lane_i == t), obs_ref[t], tile)
    params_v[r] = tile

    for v in range(STATES // 8):
        spread = jnp.zeros((8, 1), F32)
        for part in range(2):
            g = jnp.broadcast_to(gains_ref[0:1, part * 128 : part * 128 + 128], (8, 128))
            spread = spread + jnp.sum(
                jnp.where(lane_i + part * 128 == row_i + v * 8, g, F32(0.0)), axis=1, keepdims=True
            )
        g = jnp.broadcast_to(spread, (8, 128))
        gain_rows[pl.ds(v * 8, 8), :] = g
        keep[0, pl.ds(v * 8, 8), :] = jnp.ones((8, 128), F32)
        keep[1, pl.ds(v * 8, 8), :] = 1.0 - g

    pl.semaphore_wait(barrier, (ring - 1) + (nx - 1) + (nz - 1))

    par = []
    for k in range(1, ring):
        c = send(params_v.at[r], params_v.at[r], par_s.at[k], par_r.at[k], ring_dev(k))
        c.start()
        par.append(c)

    def load_state(ref_q):
        return (
            [ref_q[pl.ds(v * 8, 8), :] for v in range(VREGS)],
            [ref_q[pl.ds(SIDE + v * 8, 8), :] for v in range(VREGS)],
        )

    def own_w(t):
        s = seg_ref[t]
        return [table_ref[s, c] for c in range(CABLES)]

    ups = {}
    for f in range(tiles):
        loads[f].wait()

        def one(t, carry, f=f):
            q, p = list(carry[:VREGS]), list(carry[VREGS:])
            q, p = leap(rows, q, p, own_w(t))
            o = obs_ref[t].astype(F32)
            new = []
            for v, pred in enumerate(q + p):
                inn = mb[f, t, pl.ds(v * 8, 8), :] - pred
                new.append(pred + (o * gain_rows[pl.ds(v * 8, 8), :]) * inn)
            return tuple(new)

        q, p = load_state(x0b.at[:, pl.ds(f * 128, 128)])
        state = lax.fori_loop(0, here, one, tuple(q + p))
        q, p = list(state[:VREGS]), list(state[VREGS:])
        for half in range(2):
            packed = pack(rows, q, p, half)
            for v in range(VREGS):
                bpack[2 * f + half, pl.ds(v * 8, 8), :] = packed[v]
    for k in range(1, ring):
        peer = lax.rem(r + k, ring)
        c = send(bpack.at[peer], bin_.at[r], up_s.at[k], up_r.at[k], ring_dev(k))
        c.start()
        ups[k] = c
    own = pltpu.make_async_copy(bpack.at[r], bin_.at[r], loc_sem.at[1])
    own.start()

    for c in par:
        c.wait()
    ints = pltpu.make_async_copy(params_v, params_s, loc_sem.at[2])
    ints.start()
    ints.wait()

    def step_free(carry, j, t):
        q, p = list(carry[:VREGS]), list(carry[VREGS:])
        s = params_s[j, 0, t]
        o = params_s[j, 1, t]
        q, p = leap(rows, q, p, [table_ref[s, c] for c in range(CABLES)])
        return tuple(a * keep[o, pl.ds(v * 8, 8), :] for v, a in enumerate(q + p))

    def block_free(carry, j):
        return lax.fori_loop(0, here, lambda t, s: step_free(s, j, t), carry)

    col = lane_i + core * 128
    state = tuple(jnp.where(col == row_i + v * 8, F32(1.0), F32(0.0)) for v in range(2 * VREGS))
    state = lax.fori_loop(0, ring, lambda j, s: block_free(s, j), state)
    for v in range(2 * VREGS):
        maps[x, pl.ds(v * 8, 8), lanes(core)] = state[v]
    mine = maps.at[x, :, lanes(core)]
    mate = me + 1 - 2 * core
    mxs = []
    for k in range(1, nx):
        c = send(mine, mine, mx_s.at[k], mx_r.at[k], x_dev(k))
        c.start()
        mxs.append(c)
    mps = [send(mine, mine, mp_s.at[0], mp_r.at[0], mate)]
    mps[0].start()

    for k in range(1, ring):
        ups[k].wait()
    own.wait()

    def unpack(ref):
        a = [ref[pl.ds(v * 8, 8), :] for v in range(VREGS)]
        return a, [pltpu.roll(v, 64, 1) for v in a]

    q, p = unpack(bin_.at[0])

    def rise(j, carry):
        carry = block_free(carry, j)
        q, p = unpack(bin_.at[j])
        return tuple(a + b for a, b in zip(carry, q + p))

    state = lax.fori_loop(1, ring, rise, tuple(q + p))
    packed = pack(rows, list(state[:VREGS]), list(state[VREGS:]), 0)
    for v in range(VREGS):
        xin[x, pl.ds(v * 8, 8), :] = packed[v]
    xs = []
    for k in range(1, nx):
        c = send(xin.at[x], xin.at[x], x_s.at[k], x_r.at[k], x_dev(k))
        c.start()
        xs.append(c)

    for k in range(1, nx):
        mxs[k - 1].wait()
        there = lax.rem(x + nx - k, nx)
        src = maps.at[there, :, lanes(core)]
        c = send(src, src, mp_s.at[k], mp_r.at[k], mate)
        c.start()
        mps.append(c)
    for c in mps:
        c.wait()

    def mm(a, b):
        return jnp.dot(a, b, precision=lax.Precision.HIGHEST, preferred_element_type=F32)

    pad = jnp.zeros((256 - STATES, 128), F32)

    row2 = lax.broadcasted_iota(jnp.int32, (256, 256), 0)
    col2 = lax.broadcasted_iota(jnp.int32, (256, 256), 1)
    prefix[0] = jnp.where(row2 == col2, F32(1.0), F32(0.0))
    for i in range(nx):
        prefix[i + 1, 0:STATES, :] = mm(maps[i], prefix[i])
        prefix[i + 1, STATES:256, :] = jnp.zeros((256 - STATES, 256), F32)

    for c in xs:
        c.wait()
    sums[0] = jnp.zeros((256, 128), F32)
    for i in range(nx):
        q, p = unpack(xin.at[i])
        b = jnp.concatenate(q + p, axis=0)
        if i:
            b = b + mm(maps[i], sums[i])
        sums[i + 1, 0:STATES, :] = b
        sums[i + 1, STATES:256, :] = pad

    zcopy = send(zout, zin, z_s.at[0], z_r.at[0], z_dev(1))
    start[...] = jnp.zeros_like(start)

    @pl.when(z > 0)
    def _():
        zcopy.wait_recv()
        q, p = unpack(zin)
        for v, a in enumerate(q + p):
            start[pl.ds(v * 8, 8), :] = a

    @pl.when(z < nz - 1)
    def _():
        s = mm(prefix[nx, 0:STATES, :], start[...]) + sums[nx, 0:STATES, :]
        q = [s[v * 8 : v * 8 + 8] for v in range(VREGS)]
        p = [s[SIDE + v * 8 : SIDE + v * 8 + 8] for v in range(VREGS)]
        for v, a in enumerate(pack(rows, q, p, 0)):
            zout[pl.ds(v * 8, 8), :] = a
        zcopy.start()
        zcopy.wait_send()

    start[0:STATES, :] = mm(prefix[x, 0:STATES, :], start[...]) + sums[x, 0:STATES, :]

    q, p = load_state(start)

    def put(carry, j):
        for v, a in enumerate(pack(rows, list(carry[:VREGS]), list(carry[VREGS:]), 0)):
            sout[j, pl.ds(v * 8, 8), :] = a

    put(tuple(q + p), 0)

    def fall(j, carry):
        carry = block_free(carry, j)
        q, p = unpack(bin_.at[j])
        carry = tuple(a + b for a, b in zip(carry, q + p))
        put(carry, j + 1)
        return carry

    lax.fori_loop(0, ring - 1, fall, tuple(q + p))
    downs = []
    for k in range(1, ring):
        peer = lax.rem(r + k, ring)
        c = send(sout.at[peer], sin.at[r], dn_s.at[k], dn_r.at[k], ring_dev(k))
        c.start()
        downs.append(c)
    own = pltpu.make_async_copy(sout.at[r], sin.at[r], loc_sem.at[3])
    own.start()
    for c in downs:
        c.wait()
    own.wait()

    stores = []
    power_rows = []
    for f in range(tiles):
        a = [sin[2 * f, pl.ds(v * 8, 8), :] for v in range(VREGS)]
        b = [sin[2 * f + 1, pl.ds(v * 8, 8), :] for v in range(VREGS)]
        q = [jnp.where(rows.low, i, pltpu.roll(j, 64, 1)) for i, j in zip(a, b)]
        p = [jnp.where(rows.low, pltpu.roll(i, 64, 1), j) for i, j in zip(a, b)]
        q0, p0 = load_state(x0b.at[:, pl.ds(f * 128, 128)])
        q, p = [a + b for a, b in zip(q, q0)], [a + b for a, b in zip(p, p0)]

        def one(t, carry, f=f):
            q, p = list(carry[:VREGS]), list(carry[VREGS : 2 * VREGS])
            q, p = leap(rows, q, p, own_w(t))
            o = obs_ref[t].astype(F32)
            new = []
            squares = []
            for v, pred in enumerate(q + p):
                inn = mb[f, t, pl.ds(v * 8, 8), :] - pred
                squares.append(inn * inn)
                state = pred + (o * gain_rows[pl.ds(v * 8, 8), :]) * inn
                mb[f, t, pl.ds(v * 8, 8), :] = state
                new.append(state)
            while len(squares) > 1:
                squares = [a + b for a, b in zip(squares[::2], squares[1::2])] + (
                    [squares[-1]] if len(squares) % 2 else []
                )
            return (*new, carry[-1] + o * squares[0])

        state = lax.fori_loop(0, here, one, (*q, *p, rows.zero))
        power_rows.append(jnp.sum(state[-1], axis=0, keepdims=True))
        c = pltpu.make_async_copy(mb.at[f], out_hbm.at[:, :, pl.ds(f * 128, 128)], out_sem.at[f])
        c.start()
        stores.append(c)

    power = jnp.concatenate(power_rows + [jnp.zeros((8 - tiles, 128), F32)], axis=0)
    slot = 0
    for count, place, device in ((ring, r, ring_dev), (nx, x, x_dev), (nz, z, z_dev)):
        powers[slot + place] = power
        copies = []
        for k in range(1, count):
            ref = powers.at[slot + place]
            c = send(ref, ref, pw_s.at[slot + k], pw_r.at[slot + k], device(k))
            c.start()
            copies.append(c)
        for c in copies:
            c.wait()
        power = powers[slot]
        for k in range(1, count):
            power = power + powers[slot + k]
        slot += count
    total_steps = here * ring * nx * nz
    power_ref[...] = power[0:tiles] / F32(total_steps * STATES)
    for c in stores:
        c.wait()


def local(dims, measurements, observed, segment_ids, courant_table, filter_gains, initial_state):
    here, _, runs = measurements.shape
    nz, nx, ny = dims
    ring = ny * CORES
    tiles = runs // 128
    gains = jnp.pad(filter_gains, (0, 256 - STATES)).reshape(1, 256)
    smem = pl.BlockSpec(memory_space=pltpu.SMEM)
    vmem = pl.BlockSpec(memory_space=pltpu.VMEM)
    hbm = pl.BlockSpec(memory_space=pl.ANY)
    dma = pltpu.SemaphoreType.DMA
    packed = (SIDE, 128)
    filtered, power = pl.pallas_call(
        functools.partial(kernel, dims, runs, here),
        out_shape=(
            jax.ShapeDtypeStruct(measurements.shape, F32),
            jax.ShapeDtypeStruct((tiles, 128), F32),
        ),
        in_specs=[smem, smem, smem, vmem, hbm, hbm],
        out_specs=(hbm, vmem),
        scratch_shapes=[
            pltpu.VMEM((tiles, here, STATES, 128), F32),
            pltpu.VMEM((STATES, runs), F32),
            pltpu.VMEM((STATES, 128), F32),
            pltpu.VMEM((2, STATES, 128), F32),
            pltpu.VMEM((ring, 8, 128), jnp.int32),
            pltpu.SMEM((ring, 8, 128), jnp.int32),
            pltpu.VMEM((ring, *packed), F32),
            pltpu.VMEM((ring, *packed), F32),
            pltpu.VMEM((nx, STATES, 256), F32),
            pltpu.VMEM((nx + 1, 256, 256), F32),
            pltpu.VMEM((nx, *packed), F32),
            pltpu.VMEM((nx + 1, 256, 128), F32),
            pltpu.VMEM(packed, F32),
            pltpu.VMEM(packed, F32),
            pltpu.VMEM((256, 128), F32),
            pltpu.VMEM((ring, *packed), F32),
            pltpu.VMEM((ring, *packed), F32),
            pltpu.VMEM((ring + nx + nz, 8, 128), F32),
            dma((tiles,)),
            dma((tiles,)),
            dma((4,)),
            dma((ring,)),
            dma((ring,)),
            dma((ring,)),
            dma((ring,)),
            dma((nx,)),
            dma((nx,)),
            dma((nx,)),
            dma((nx,)),
            dma((nx,)),
            dma((nx,)),
            dma((1,)),
            dma((1,)),
            dma((ring,)),
            dma((ring,)),
            dma((ring + nx + nz,)),
            dma((ring + nx + nz,)),
        ],
        compiler_params=pltpu.CompilerParams(
            collective_id=0, has_side_effects=True, vmem_limit_bytes=48 << 20
        ),
    )(segment_ids, observed, courant_table, gains, measurements, initial_state)
    return filtered, power.reshape(runs)


def solution(mesh):
    dims = torus_of(mesh.size)
    in_specs = (P("tm", None, None), P("tm"), P("tm"), P(), P(), P())
    out_specs = (P("tm", None, None), P())
    return jax.shard_map(
        functools.partial(local, dims), mesh=mesh, in_specs=in_specs, out_specs=out_specs, check_vma=False
    )
```

```python
import functools

import jax
import jax.numpy as jnp
from jax import lax
from jax.experimental import pallas as pl
from jax.experimental.pallas import tpu as pltpu
from jax.sharding import PartitionSpec as P

CABLES = 4
HALF = 24
SIDE = CABLES * HALF
STATES = 2 * SIDE
SEGS = 32
PAYLOAD = 0.3
CORES = 2
MESH = pl.DeviceIdType.MESH
VREGS = SIDE // 8
F32 = jnp.float32


def torus_of(devices):
    return {128: (4, 4, 4), 16: (2, 2, 2)}[devices]


def lanes(tile):
    return pl.ds(pl.multiple_of(tile * 128, 128), 128)


class Rows:
    def __init__(self):
        row = lax.broadcasted_iota(jnp.int32, (8, 128), 0)
        self.first = row == 0
        self.last = row == 7
        self.pay = jnp.where(self.last, F32(PAYLOAD), F32(0.0))
        self.zero = jnp.zeros((8, 128), F32)
        self.low = lax.broadcasted_iota(jnp.int32, (8, 128), 1) < 64


def node(v):
    return pl.ds(HALF * (v // 3) + v % 3, 8, stride=3)


def leap(rows, q, p, w):
    total = (q[2] + q[5]) + (q[8] + q[11])
    wrap = [jnp.where(rows.first, rows.zero, pltpu.roll(q[3 * c + 2], 1, 0)) for c in range(CABLES)]
    new_p, u = [], []
    for v in range(VREGS):
        d = q[v] - (q[v - 1] if v % 3 else wrap[v // 3])
        if v % 3 == 2:
            d = d - rows.pay * (total - q[v])
        new_p.append(p[v] + w[v // 3] * d)
        u.append(w[v // 3] * new_p[v])
    wrap = [jnp.where(rows.last, rows.zero, pltpu.roll(u[3 * c], 7, 0)) for c in range(CABLES)]
    total = (u[2] + u[5]) + (u[8] + u[11])
    new_q = []
    for v in range(VREGS):
        e = u[v] - (u[v + 1] if v % 3 < 2 else wrap[v // 3])
        if v % 3 == 2:
            e = e - rows.pay * (total - u[v])
        new_q.append(q[v] - e)
    return new_q, new_p


def pack(rows, q, p, half):
    if half == 0:
        return [jnp.where(rows.low, a, pltpu.roll(b, 64, 1)) for a, b in zip(q, p)]
    return [jnp.where(rows.low, pltpu.roll(a, 64, 1), b) for a, b in zip(q, p)]


def kernel(
    dims, runs, steps,
    seg_ref, obs_ref, table_ref, gains_ref, m_hbm, x0_hbm,
    out_hbm, power_ref,
    mb, x0b, tab, phi, phi_out, starts, firsts, gain_rows, keep, params_v, params_s, bpack, bin_, maps, prefix, xin, sums, zin, zout,
    start, sout, sin, powers,
    m_sem, out_sem, loc_sem,
    par_s, par_r, up_s, up_r, mx_s, mx_r, mp_s, mp_r, x_s, x_r, z_s, z_r, dn_s, dn_r, st_s, st_r, ph_s, ph_r, pw_s, pw_r,
):
    nz, nx, ny = dims
    ring = ny * CORES
    here = steps
    tiles = runs // 128
    me = lax.axis_index("tm")
    r = lax.rem(me, ring)
    core = lax.rem(me, CORES)
    x = lax.rem(me // ring, nx)
    z = me // (ring * nx)
    base = me - r
    rows = Rows()

    def ring_dev(k):
        return base + lax.rem(r + k, ring)

    def x_dev(k):
        return (z * nx + lax.rem(x + k, nx)) * ring + r

    def z_dev(k):
        return (lax.rem(z + k, nz) * nx + x) * ring + r

    def send(src, dst, ssem, rsem, dev):
        return pltpu.make_async_remote_copy(
            src_ref=src, dst_ref=dst, send_sem=ssem, recv_sem=rsem, device_id=(dev,), device_id_type=MESH
        )

    loads = []
    for f in range(tiles):
        c = pltpu.make_async_copy(m_hbm.at[:, :, pl.ds(f * 128, 128)], mb.at[f], m_sem.at[f])
        c.start()
        loads.append(c)

    barrier = pltpu.get_barrier_semaphore()
    for k in range(1, ring):
        pl.semaphore_signal(barrier, inc=1, device_id=(ring_dev(k),), device_id_type=MESH)
    for k in range(1, nx):
        pl.semaphore_signal(barrier, inc=1, device_id=(x_dev(k),), device_id_type=MESH)
    for k in range(1, nz):
        pl.semaphore_signal(barrier, inc=1, device_id=(z_dev(k),), device_id_type=MESH)

    @pl.when(me == 0)
    def _():
        copies = []
        for f in range(tiles):
            c = pltpu.make_async_copy(x0_hbm.at[:, pl.ds(f * 128, 128)], x0b.at[f], loc_sem.at[0])
            c.start()
            copies.append(c)
        for c in copies:
            c.wait()

    @pl.when(me > 0)
    def _():
        x0b[...] = jnp.zeros_like(x0b)

    row_i = lax.broadcasted_iota(jnp.int32, (8, 128), 0)
    lane_i = lax.broadcasted_iota(jnp.int32, (8, 128), 1)
    tile = jnp.zeros((8, 128), jnp.int32)
    for t in range(here):
        tile = jnp.where((row_i == 0) & (lane_i == t), seg_ref[t], tile)
        tile = jnp.where((row_i == 1) & (lane_i == t), obs_ref[t], tile)
    params_v[r] = tile

    for v in range(STATES // 8):
        spread = jnp.zeros((8, 1), F32)
        for part in range(2):
            g = jnp.broadcast_to(gains_ref[0:1, part * 128 : part * 128 + 128], (8, 128))
            spread = spread + jnp.sum(
                jnp.where(lane_i + part * 128 == row_i * 3 + (HALF * (v // 3) + v % 3), g, F32(0.0)), axis=1, keepdims=True
            )
        g = jnp.broadcast_to(spread, (8, 128))
        gain_rows[pl.ds(v * 8, 8), :] = g
        keep[0, pl.ds(v * 8, 8), :] = jnp.ones((8, 128), F32)
        keep[1, pl.ds(v * 8, 8), :] = 1.0 - g

    for c in range(CABLES):
        tab[c] = jnp.broadcast_to(table_ref[:, c : c + 1], (SEGS, 128))

    def spread_w(s):
        return [jnp.broadcast_to(tab[c, pl.ds(s, 1), :], (8, 128)) for c in range(CABLES)]

    pl.semaphore_wait(barrier, (ring - 1) + (nx - 1) + (nz - 1))

    par = []
    for k in range(1, ring):
        c = send(params_v.at[r], params_v.at[r], par_s.at[k], par_r.at[k], ring_dev(k))
        c.start()
        par.append(c)

    def load_state(ref_q):
        return (
            [ref_q[pl.ds(v * 8, 8), :] for v in range(VREGS)],
            [ref_q[pl.ds(SIDE + v * 8, 8), :] for v in range(VREGS)],
        )

    def load_first(f):
        return (
            [x0b[f, node(v), :] for v in range(VREGS)],
            [x0b[f, node(VREGS + v), :] for v in range(VREGS)],
        )

    def own_w(t):
        return spread_w(seg_ref[t])

    ups = {}
    for f in range(tiles):
        loads[f].wait()

        def one(t, carry, f=f):
            q, p = list(carry[:VREGS]), list(carry[VREGS:])
            q, p = leap(rows, q, p, own_w(t))
            o = obs_ref[t].astype(F32)
            new = []
            for v, pred in enumerate(q + p):
                inn = mb[f, t, node(v), :] - pred
                new.append(pred + (o * gain_rows[pl.ds(v * 8, 8), :]) * inn)
            return tuple(new)

        q, p = load_first(f)
        state = lax.fori_loop(0, here, one, tuple(q + p), unroll=2)
        q, p = list(state[:VREGS]), list(state[VREGS:])
        for half in range(2):
            packed = pack(rows, q, p, half)
            for v in range(VREGS):
                bpack[2 * f + half, pl.ds(v * 8, 8), :] = packed[v]
    for k in range(1, ring):
        peer = lax.rem(r + k, ring)
        c = send(bpack.at[peer], bin_.at[r], up_s.at[k], up_r.at[k], ring_dev(k))
        c.start()
        ups[k] = c
    own = pltpu.make_async_copy(bpack.at[r], bin_.at[r], loc_sem.at[1])
    own.start()

    for c in par:
        c.wait()
    ints = pltpu.make_async_copy(params_v, params_s, loc_sem.at[2])
    ints.start()
    ints.wait()

    def step_free(carry, j, t):
        q, p = list(carry[:VREGS]), list(carry[VREGS:])
        s = params_s[j, 0, t]
        o = params_s[j, 1, t]
        q, p = leap(rows, q, p, spread_w(s))
        return tuple(a * keep[o, pl.ds(v * 8, 8), :] for v, a in enumerate(q + p))

    def block_free(carry, j):
        return lax.fori_loop(0, here, lambda t, s: step_free(s, j, t), carry, unroll=4)

    col = lane_i + core * 128
    state = tuple(jnp.where(col == row_i + v * 8, F32(1.0), F32(0.0)) for v in range(2 * VREGS))
    mate = me + 1 - 2 * core
    mate_r = r + 1 - 2 * core

    def climb(j, carry):
        @pl.when(j == r)
        def _():
            for v, a in enumerate(carry):
                phi[pl.ds(v * 8, 8), lanes(core)] = a

        @pl.when(j == mate_r)
        def _():
            for v, a in enumerate(carry):
                phi_out[pl.ds(v * 8, 8), :] = a

        return block_free(carry, j)

    state = lax.fori_loop(0, ring, climb, state)
    for v in range(2 * VREGS):
        maps[x, pl.ds(v * 8, 8), lanes(core)] = state[v]
    mine = maps.at[x, :, lanes(core)]
    mxs = []
    for k in range(1, nx):
        c = send(mine, mine, mx_s.at[k], mx_r.at[k], x_dev(k))
        c.start()
        mxs.append(c)
    mps = [send(mine, mine, mp_s.at[0], mp_r.at[0], mate)]
    mps[0].start()

    phic = send(phi_out, phi.at[:, lanes(core)], ph_s.at[0], ph_r.at[0], mate)
    phic.start()

    for k in range(1, ring):
        ups[k].wait()
    own.wait()

    def unpack(ref):
        a = [ref[pl.ds(v * 8, 8), :] for v in range(VREGS)]
        return a, [pltpu.roll(v, 64, 1) for v in a]

    def put(carry, j):
        for v, a in enumerate(pack(rows, list(carry[:VREGS]), list(carry[VREGS:]), 0)):
            sout[j, pl.ds(v * 8, 8), :] = a

    for v in range(VREGS):
        sout[0, pl.ds(v * 8, 8), :] = rows.zero
    q, p = unpack(bin_.at[0])

    def rise(j, carry):
        put(carry, j)
        carry = block_free(carry, j)
        q, p = unpack(bin_.at[j])
        return tuple(a + b for a, b in zip(carry, q + p))

    state = lax.fori_loop(1, ring, rise, tuple(q + p))
    packed = pack(rows, list(state[:VREGS]), list(state[VREGS:]), 0)
    for v in range(VREGS):
        xin[x, pl.ds(v * 8, 8), :] = packed[v]
    xs = []
    for k in range(1, nx):
        c = send(xin.at[x], xin.at[x], x_s.at[k], x_r.at[k], x_dev(k))
        c.start()
        xs.append(c)

    downs = []
    for k in range(1, ring):
        peer = lax.rem(r + k, ring)
        c = send(sout.at[peer], sin.at[r], dn_s.at[k], dn_r.at[k], ring_dev(k))
        c.start()
        downs.append(c)
    own_down = pltpu.make_async_copy(sout.at[r], sin.at[r], loc_sem.at[3])
    own_down.start()

    for k in range(1, nx):
        mxs[k - 1].wait()
        there = lax.rem(x + nx - k, nx)
        src = maps.at[there, :, lanes(core)]
        c = send(src, src, mp_s.at[k], mp_r.at[k], mate)
        c.start()
        mps.append(c)
    for c in mps:
        c.wait()

    def mm(a, b):
        return jnp.dot(a, b, precision=lax.Precision.HIGHEST, preferred_element_type=F32)

    pad = jnp.zeros((256 - STATES, 128), F32)

    row2 = lax.broadcasted_iota(jnp.int32, (256, 256), 0)
    col2 = lax.broadcasted_iota(jnp.int32, (256, 256), 1)
    prefix[0] = jnp.where(row2 == col2, F32(1.0), F32(0.0))
    for i in range(nx):
        prefix[i + 1, 0:STATES, :] = mm(maps[i], prefix[i])
        prefix[i + 1, STATES:256, :] = jnp.zeros((256 - STATES, 256), F32)

    for c in xs:
        c.wait()
    sums[0] = jnp.zeros((256, 128), F32)
    for i in range(nx):
        q, p = unpack(xin.at[i])
        b = jnp.concatenate(q + p, axis=0)
        if i:
            b = b + mm(maps[i], sums[i])
        sums[i + 1, 0:STATES, :] = b
        sums[i + 1, STATES:256, :] = pad

    zcopy = send(zout, zin, z_s.at[0], z_r.at[0], z_dev(1))
    start[...] = jnp.zeros_like(start)

    @pl.when(z > 0)
    def _():
        zcopy.wait_recv()
        q, p = unpack(zin)
        for v, a in enumerate(q + p):
            start[pl.ds(v * 8, 8), :] = a

    @pl.when(z < nz - 1)
    def _():
        s = mm(prefix[nx, 0:STATES, :], start[...]) + sums[nx, 0:STATES, :]
        q = [s[v * 8 : v * 8 + 8] for v in range(VREGS)]
        p = [s[SIDE + v * 8 : SIDE + v * 8 + 8] for v in range(VREGS)]
        for v, a in enumerate(pack(rows, q, p, 0)):
            zout[pl.ds(v * 8, 8), :] = a
        zcopy.start()
        zcopy.wait_send()

    start[0:STATES, :] = mm(prefix[x, 0:STATES, :], start[...]) + sums[x, 0:STATES, :]

    q, p = load_state(start)
    for v, a in enumerate(pack(rows, q, p, 0)):
        starts[r, pl.ds(v * 8, 8), :] = a
    sts = []
    for k in range(1, ring):
        c = send(starts.at[r], starts.at[r], st_s.at[k], st_r.at[k], ring_dev(k))
        c.start()
        sts.append(c)
    phic.wait()
    for c in downs:
        c.wait()
    own_down.wait()
    for c in sts:
        c.wait()

    def merge(ref, f):
        a = [ref[2 * f, pl.ds(v * 8, 8), :] for v in range(VREGS)]
        b = [ref[2 * f + 1, pl.ds(v * 8, 8), :] for v in range(VREGS)]
        q = [jnp.where(rows.low, i, pltpu.roll(j, 64, 1)) for i, j in zip(a, b)]
        p = [jnp.where(rows.low, pltpu.roll(i, 64, 1), j) for i, j in zip(a, b)]
        return q, p

    for f in range(tiles):
        q, p = merge(starts, f)
        for v, a in enumerate(q + p):
            firsts[pl.ds(v * 8, 8), pl.ds(f * 128, 128)] = a
    firsts[STATES:256, :] = jnp.zeros((256 - STATES, runs), F32)
    firsts[0:STATES, :] = mm(phi[...], firsts[...])

    stores = []
    power_rows = []
    for f in range(tiles):
        q, p = merge(sin, f)
        q1, p1 = load_state(firsts.at[:, pl.ds(f * 128, 128)])
        q, p = [a + b for a, b in zip(q, q1)], [a + b for a, b in zip(p, p1)]
        q0, p0 = load_first(f)
        q, p = [a + b for a, b in zip(q, q0)], [a + b for a, b in zip(p, p0)]

        def one(t, carry, f=f):
            q, p = list(carry[:VREGS]), list(carry[VREGS : 2 * VREGS])
            q, p = leap(rows, q, p, own_w(t))
            o = obs_ref[t].astype(F32)
            new = []
            squares = []
            for v, pred in enumerate(q + p):
                inn = mb[f, t, node(v), :] - pred
                squares.append(inn * inn)
                state = pred + (o * gain_rows[pl.ds(v * 8, 8), :]) * inn
                mb[f, t, node(v), :] = state
                new.append(state)
            while len(squares) > 1:
                squares = [a + b for a, b in zip(squares[::2], squares[1::2])] + (
                    [squares[-1]] if len(squares) % 2 else []
                )
            return (*new, carry[-1] + o * squares[0])

        state = lax.fori_loop(0, here, one, (*q, *p, rows.zero), unroll=2)
        power_rows.append(jnp.sum(state[-1], axis=0, keepdims=True))
        c = pltpu.make_async_copy(mb.at[f], out_hbm.at[:, :, pl.ds(f * 128, 128)], out_sem.at[f])
        c.start()
        stores.append(c)

    power = jnp.concatenate(power_rows + [jnp.zeros((8 - tiles, 128), F32)], axis=0)
    slot = 0
    for count, place, device in ((ring, r, ring_dev), (nx, x, x_dev), (nz, z, z_dev)):
        powers[slot + place] = power
        copies = []
        for k in range(1, count):
            ref = powers.at[slot + place]
            c = send(ref, ref, pw_s.at[slot + k], pw_r.at[slot + k], device(k))
            c.start()
            copies.append(c)
        for c in copies:
            c.wait()
        power = powers[slot]
        for k in range(1, count):
            power = power + powers[slot + k]
        slot += count
    total_steps = here * ring * nx * nz
    power_ref[...] = power[0:tiles] / F32(total_steps * STATES)
    for c in stores:
        c.wait()


def local(dims, measurements, observed, segment_ids, courant_table, filter_gains, initial_state):
    here, _, runs = measurements.shape
    nz, nx, ny = dims
    ring = ny * CORES
    tiles = runs // 128
    gains = jnp.pad(filter_gains, (0, 256 - STATES)).reshape(1, 256)
    smem = pl.BlockSpec(memory_space=pltpu.SMEM)
    vmem = pl.BlockSpec(memory_space=pltpu.VMEM)
    hbm = pl.BlockSpec(memory_space=pl.ANY)
    dma = pltpu.SemaphoreType.DMA
    packed = (SIDE, 128)
    filtered, power = pl.pallas_call(
        functools.partial(kernel, dims, runs, here),
        out_shape=(
            jax.ShapeDtypeStruct(measurements.shape, F32),
            jax.ShapeDtypeStruct((tiles, 128), F32),
        ),
        in_specs=[smem, smem, vmem, vmem, hbm, hbm],
        out_specs=(hbm, vmem),
        scratch_shapes=[
            pltpu.VMEM((tiles, here, STATES, 128), F32),
            pltpu.VMEM((tiles, STATES, 128), F32),
            pltpu.VMEM((CABLES, SEGS, 128), F32),
            pltpu.VMEM((STATES, 256), F32),
            pltpu.VMEM((STATES, 128), F32),
            pltpu.VMEM((ring, *packed), F32),
            pltpu.VMEM((256, runs), F32),
            pltpu.VMEM((STATES, 128), F32),
            pltpu.VMEM((2, STATES, 128), F32),
            pltpu.VMEM((ring, 8, 128), jnp.int32),
            pltpu.SMEM((ring, 8, 128), jnp.int32),
            pltpu.VMEM((ring, *packed), F32),
            pltpu.VMEM((ring, *packed), F32),
            pltpu.VMEM((nx, STATES, 256), F32),
            pltpu.VMEM((nx + 1, 256, 256), F32),
            pltpu.VMEM((nx, *packed), F32),
            pltpu.VMEM((nx + 1, 256, 128), F32),
            pltpu.VMEM(packed, F32),
            pltpu.VMEM(packed, F32),
            pltpu.VMEM((256, 128), F32),
            pltpu.VMEM((ring, *packed), F32),
            pltpu.VMEM((ring, *packed), F32),
            pltpu.VMEM((ring + nx + nz, 8, 128), F32),
            dma((tiles,)),
            dma((tiles,)),
            dma((4,)),
            dma((ring,)),
            dma((ring,)),
            dma((ring,)),
            dma((ring,)),
            dma((nx,)),
            dma((nx,)),
            dma((nx,)),
            dma((nx,)),
            dma((nx,)),
            dma((nx,)),
            dma((1,)),
            dma((1,)),
            dma((ring,)),
            dma((ring,)),
            dma((ring,)),
            dma((ring,)),
            dma((1,)),
            dma((1,)),
            dma((ring + nx + nz,)),
            dma((ring + nx + nz,)),
        ],
        compiler_params=pltpu.CompilerParams(
            collective_id=0, has_side_effects=True, vmem_limit_bytes=48 << 20
        ),
    )(segment_ids, observed, courant_table, gains, measurements, initial_state)
    return filtered, power.reshape(runs)


def solution(mesh):
    dims = torus_of(mesh.size)
    in_specs = (P("tm", None, None), P("tm"), P("tm"), P(), P(), P())
    out_specs = (P("tm", None, None), P())
    return jax.shard_map(
        functools.partial(local, dims), mesh=mesh, in_specs=in_specs, out_specs=out_specs, check_vma=False
    )
```

```python
import functools

import jax
import jax.numpy as jnp
from jax import lax
from jax.experimental import pallas as pl
from jax.experimental.pallas import tpu as pltpu
from jax.sharding import PartitionSpec as P

CABLES = 4
HALF = 24
SIDE = CABLES * HALF
STATES = 2 * SIDE
SEGS = 32
PAYLOAD = 0.3
CORES = 2
MESH = pl.DeviceIdType.MESH
VREGS = SIDE // 8
F32 = jnp.float32


def torus_of(devices):
    return {128: (4, 4, 4), 16: (2, 2, 2)}[devices]


def lanes(tile):
    return pl.ds(pl.multiple_of(tile * 128, 128), 128)


class Rows:
    def __init__(self):
        row = lax.broadcasted_iota(jnp.int32, (8, 128), 0)
        self.first = row == 0
        self.last = row == 7
        self.pay = jnp.where(self.last, F32(PAYLOAD), F32(0.0))
        self.zero = jnp.zeros((8, 128), F32)
        self.low = lax.broadcasted_iota(jnp.int32, (8, 128), 1) < 64


def node(v):
    return pl.ds(HALF * (v // 3) + v % 3, 8, stride=3)


def leap(rows, q, p, w):
    total = (q[2] + q[5]) + (q[8] + q[11])
    wrap = [jnp.where(rows.first, rows.zero, pltpu.roll(q[3 * c + 2], 1, 0)) for c in range(CABLES)]
    new_p, u = [], []
    for v in range(VREGS):
        d = q[v] - (q[v - 1] if v % 3 else wrap[v // 3])
        if v % 3 == 2:
            d = d - rows.pay * (total - q[v])
        new_p.append(p[v] + w[v // 3] * d)
        u.append(w[v // 3] * new_p[v])
    wrap = [jnp.where(rows.last, rows.zero, pltpu.roll(u[3 * c], 7, 0)) for c in range(CABLES)]
    total = (u[2] + u[5]) + (u[8] + u[11])
    new_q = []
    for v in range(VREGS):
        e = u[v] - (u[v + 1] if v % 3 < 2 else wrap[v // 3])
        if v % 3 == 2:
            e = e - rows.pay * (total - u[v])
        new_q.append(q[v] - e)
    return new_q, new_p


def pack(rows, q, p, half):
    if half == 0:
        return [jnp.where(rows.low, a, pltpu.roll(b, 64, 1)) for a, b in zip(q, p)]
    return [jnp.where(rows.low, pltpu.roll(a, 64, 1), b) for a, b in zip(q, p)]


def kernel(
    dims, runs, steps,
    seg_hbm, obs_hbm, table_hbm, gains_hbm, m_hbm, x0_hbm,
    out_hbm, power_ref,
    seg_ref, obs_ref, table_ref, gains_ref, small_sem, mb, x0b, tab, phi, phi_out, starts, firsts, gain_rows, keep, params_v, params_s, bpack, bin_, maps, prefix, xin, sums, zin, zout,
    start, sout, sin, powers,
    m_sem, out_sem, loc_sem,
    par_s, par_r, up_s, up_r, mx_s, mx_r, mp_s, mp_r, x_s, x_r, z_s, z_r, dn_s, dn_r, st_s, st_r, ph_s, ph_r, pw_s, pw_r,
):
    nz, nx, ny = dims
    ring = ny * CORES
    here = steps
    tiles = runs // 128
    me = lax.axis_index("tm")
    r = lax.rem(me, ring)
    core = lax.rem(me, CORES)
    x = lax.rem(me // ring, nx)
    z = me // (ring * nx)
    base = me - r
    rows = Rows()

    def ring_dev(k):
        return base + lax.rem(r + k, ring)

    def x_dev(k):
        return (z * nx + lax.rem(x + k, nx)) * ring + r

    def z_dev(k):
        return (lax.rem(z + k, nz) * nx + x) * ring + r

    def send(src, dst, ssem, rsem, dev):
        return pltpu.make_async_remote_copy(
            src_ref=src, dst_ref=dst, send_sem=ssem, recv_sem=rsem, device_id=(dev,), device_id_type=MESH
        )

    smalls = []
    for i, (src, dst) in enumerate(
        ((seg_hbm, seg_ref), (obs_hbm, obs_ref), (table_hbm, table_ref), (gains_hbm, gains_ref))
    ):
        c = pltpu.make_async_copy(src, dst, small_sem.at[i])
        c.start()
        smalls.append(c)
    loads = []
    for f in range(tiles):
        c = pltpu.make_async_copy(m_hbm.at[:, :, pl.ds(f * 128, 128)], mb.at[f], m_sem.at[f])
        c.start()
        loads.append(c)

    barrier = pltpu.get_barrier_semaphore()
    for k in range(1, ring):
        pl.semaphore_signal(barrier, inc=1, device_id=(ring_dev(k),), device_id_type=MESH)
    for k in range(1, nx):
        pl.semaphore_signal(barrier, inc=1, device_id=(x_dev(k),), device_id_type=MESH)
    for k in range(1, nz):
        pl.semaphore_signal(barrier, inc=1, device_id=(z_dev(k),), device_id_type=MESH)

    @pl.when(me == 0)
    def _():
        copies = []
        for f in range(tiles):
            c = pltpu.make_async_copy(x0_hbm.at[:, pl.ds(f * 128, 128)], x0b.at[f], loc_sem.at[0])
            c.start()
            copies.append(c)
        for c in copies:
            c.wait()

    @pl.when(me > 0)
    def _():
        x0b[...] = jnp.zeros_like(x0b)

    for c in smalls:
        c.wait()

    row_i = lax.broadcasted_iota(jnp.int32, (8, 128), 0)
    lane_i = lax.broadcasted_iota(jnp.int32, (8, 128), 1)
    tile = jnp.zeros((8, 128), jnp.int32)
    for t in range(here):
        tile = jnp.where((row_i == 0) & (lane_i == t), seg_ref[t], tile)
        tile = jnp.where((row_i == 1) & (lane_i == t), obs_ref[t], tile)
    params_v[r] = tile

    gain_lanes = [
        gains_ref[0:1, 0:128],
        jnp.concatenate([gains_ref[0:1, 128:STATES], jnp.zeros((1, 256 - STATES), F32)], axis=1),
    ]
    for v in range(STATES // 8):
        spread = jnp.zeros((8, 1), F32)
        for part in range(2):
            g = jnp.broadcast_to(gain_lanes[part], (8, 128))
            spread = spread + jnp.sum(
                jnp.where(lane_i + part * 128 == row_i * 3 + (HALF * (v // 3) + v % 3), g, F32(0.0)), axis=1, keepdims=True
            )
        g = jnp.broadcast_to(spread, (8, 128))
        gain_rows[pl.ds(v * 8, 8), :] = g
        keep[0, pl.ds(v * 8, 8), :] = jnp.ones((8, 128), F32)
        keep[1, pl.ds(v * 8, 8), :] = 1.0 - g

    for c in range(CABLES):
        tab[c] = jnp.broadcast_to(table_ref[:, c : c + 1], (SEGS, 128))

    def spread_w(s):
        return [jnp.broadcast_to(tab[c, pl.ds(s, 1), :], (8, 128)) for c in range(CABLES)]

    pl.semaphore_wait(barrier, (ring - 1) + (nx - 1) + (nz - 1))

    par = []
    for k in range(1, ring):
        c = send(params_v.at[r], params_v.at[r], par_s.at[k], par_r.at[k], ring_dev(k))
        c.start()
        par.append(c)

    def load_state(ref_q):
        return (
            [ref_q[pl.ds(v * 8, 8), :] for v in range(VREGS)],
            [ref_q[pl.ds(SIDE + v * 8, 8), :] for v in range(VREGS)],
        )

    def load_first(f):
        return (
            [x0b[f, node(v), :] for v in range(VREGS)],
            [x0b[f, node(VREGS + v), :] for v in range(VREGS)],
        )

    def own_w(t):
        return spread_w(seg_ref[t])

    ups = {}
    both = 2 * VREGS
    for f0 in range(0, tiles, 2):
        loads[f0].wait()
        loads[f0 + 1].wait()

        def one(t, carry, f0=f0):
            w = own_w(t)
            o = obs_ref[t].astype(F32)
            preds = []
            for i in range(2):
                s = list(carry[i * both : (i + 1) * both])
                preds.append(leap(rows, s[:VREGS], s[VREGS:], w))
            new = [None] * (2 * both)
            for v in range(both):
                gain = o * gain_rows[pl.ds(v * 8, 8), :]
                for i, (q, p) in enumerate(preds):
                    pred = (q + p)[v]
                    new[i * both + v] = pred + gain * (mb[f0 + i, t, node(v), :] - pred)
            return tuple(new)

        first = [load_first(f0), load_first(f0 + 1)]
        state = lax.fori_loop(0, here, one, tuple(a for q, p in first for a in q + p), unroll=2)
        for i in range(2):
            s = list(state[i * both : (i + 1) * both])
            for half in range(2):
                packed = pack(rows, s[:VREGS], s[VREGS:], half)
                for v in range(VREGS):
                    bpack[2 * (f0 + i) + half, pl.ds(v * 8, 8), :] = packed[v]
    for k in range(1, ring):
        peer = lax.rem(r + k, ring)
        c = send(bpack.at[peer], bin_.at[r], up_s.at[k], up_r.at[k], ring_dev(k))
        c.start()
        ups[k] = c
    own = pltpu.make_async_copy(bpack.at[r], bin_.at[r], loc_sem.at[1])
    own.start()

    for c in par:
        c.wait()
    ints = pltpu.make_async_copy(params_v, params_s, loc_sem.at[2])
    ints.start()
    ints.wait()

    def step_free(carry, j, t):
        q, p = list(carry[:VREGS]), list(carry[VREGS:])
        s = params_s[j, 0, t]
        o = params_s[j, 1, t]
        q, p = leap(rows, q, p, spread_w(s))
        return tuple(a * keep[o, pl.ds(v * 8, 8), :] for v, a in enumerate(q + p))

    def block_free(carry, j):
        return lax.fori_loop(0, here, lambda t, s: step_free(s, j, t), carry, unroll=4)

    col = lane_i + core * 128
    state = tuple(jnp.where(col == row_i + v * 8, F32(1.0), F32(0.0)) for v in range(2 * VREGS))
    mate = me + 1 - 2 * core
    mate_r = r + 1 - 2 * core

    def climb(j, carry):
        @pl.when(j == r)
        def _():
            for v, a in enumerate(carry):
                phi[pl.ds(v * 8, 8), lanes(core)] = a

        @pl.when(j == mate_r)
        def _():
            for v, a in enumerate(carry):
                phi_out[pl.ds(v * 8, 8), :] = a

        return block_free(carry, j)

    state = lax.fori_loop(0, ring, climb, state)
    for v in range(2 * VREGS):
        maps[x, pl.ds(v * 8, 8), lanes(core)] = state[v]
    mine = maps.at[x, :, lanes(core)]
    mxs = []
    for k in range(1, nx):
        c = send(mine, mine, mx_s.at[k], mx_r.at[k], x_dev(k))
        c.start()
        mxs.append(c)
    mps = [send(mine, mine, mp_s.at[0], mp_r.at[0], mate)]
    mps[0].start()

    phic = send(phi_out, phi.at[:, lanes(core)], ph_s.at[0], ph_r.at[0], mate)
    phic.start()

    for k in range(1, ring):
        ups[k].wait()
    own.wait()

    def unpack(ref):
        a = [ref[pl.ds(v * 8, 8), :] for v in range(VREGS)]
        return a, [pltpu.roll(v, 64, 1) for v in a]

    def put(carry, j):
        for v, a in enumerate(pack(rows, list(carry[:VREGS]), list(carry[VREGS:]), 0)):
            sout[j, pl.ds(v * 8, 8), :] = a

    for v in range(VREGS):
        sout[0, pl.ds(v * 8, 8), :] = rows.zero
    q, p = unpack(bin_.at[0])

    def rise(j, carry):
        put(carry, j)
        carry = block_free(carry, j)
        q, p = unpack(bin_.at[j])
        return tuple(a + b for a, b in zip(carry, q + p))

    state = lax.fori_loop(1, ring, rise, tuple(q + p))
    packed = pack(rows, list(state[:VREGS]), list(state[VREGS:]), 0)
    for v in range(VREGS):
        xin[x, pl.ds(v * 8, 8), :] = packed[v]
    xs = []
    for k in range(1, nx):
        c = send(xin.at[x], xin.at[x], x_s.at[k], x_r.at[k], x_dev(k))
        c.start()
        xs.append(c)

    downs = []
    for k in range(1, ring):
        peer = lax.rem(r + k, ring)
        c = send(sout.at[peer], sin.at[r], dn_s.at[k], dn_r.at[k], ring_dev(k))
        c.start()
        downs.append(c)
    own_down = pltpu.make_async_copy(sout.at[r], sin.at[r], loc_sem.at[3])
    own_down.start()

    for k in range(1, nx):
        mxs[k - 1].wait()
        there = lax.rem(x + nx - k, nx)
        src = maps.at[there, :, lanes(core)]
        c = send(src, src, mp_s.at[k], mp_r.at[k], mate)
        c.start()
        mps.append(c)
    for c in mps:
        c.wait()

    def mm(a, b):
        return jnp.dot(a, b, precision=lax.Precision.HIGHEST, preferred_element_type=F32)

    pad = jnp.zeros((256 - STATES, 128), F32)

    row2 = lax.broadcasted_iota(jnp.int32, (256, 256), 0)
    col2 = lax.broadcasted_iota(jnp.int32, (256, 256), 1)
    prefix[0] = jnp.where(row2 == col2, F32(1.0), F32(0.0))
    for i in range(nx):
        prefix[i + 1, 0:STATES, :] = mm(maps[i], prefix[i])
        prefix[i + 1, STATES:256, :] = jnp.zeros((256 - STATES, 256), F32)

    for c in xs:
        c.wait()
    sums[0] = jnp.zeros((256, 128), F32)
    for i in range(nx):
        q, p = unpack(xin.at[i])
        b = jnp.concatenate(q + p, axis=0)
        if i:
            b = b + mm(maps[i], sums[i])
        sums[i + 1, 0:STATES, :] = b
        sums[i + 1, STATES:256, :] = pad

    zcopy = send(zout, zin, z_s.at[0], z_r.at[0], z_dev(1))
    start[...] = jnp.zeros_like(start)

    @pl.when(z > 0)
    def _():
        zcopy.wait_recv()
        q, p = unpack(zin)
        for v, a in enumerate(q + p):
            start[pl.ds(v * 8, 8), :] = a

    @pl.when(z < nz - 1)
    def _():
        s = mm(prefix[nx, 0:STATES, :], start[...]) + sums[nx, 0:STATES, :]
        q = [s[v * 8 : v * 8 + 8] for v in range(VREGS)]
        p = [s[SIDE + v * 8 : SIDE + v * 8 + 8] for v in range(VREGS)]
        for v, a in enumerate(pack(rows, q, p, 0)):
            zout[pl.ds(v * 8, 8), :] = a
        zcopy.start()
        zcopy.wait_send()

    start[0:STATES, :] = mm(prefix[x, 0:STATES, :], start[...]) + sums[x, 0:STATES, :]

    q, p = load_state(start)
    for v, a in enumerate(pack(rows, q, p, 0)):
        starts[r, pl.ds(v * 8, 8), :] = a
    sts = []
    for k in range(1, ring):
        c = send(starts.at[r], starts.at[r], st_s.at[k], st_r.at[k], ring_dev(k))
        c.start()
        sts.append(c)
    phic.wait()
    for c in downs:
        c.wait()
    own_down.wait()
    for c in sts:
        c.wait()

    def merge(ref, f):
        a = [ref[2 * f, pl.ds(v * 8, 8), :] for v in range(VREGS)]
        b = [ref[2 * f + 1, pl.ds(v * 8, 8), :] for v in range(VREGS)]
        q = [jnp.where(rows.low, i, pltpu.roll(j, 64, 1)) for i, j in zip(a, b)]
        p = [jnp.where(rows.low, pltpu.roll(i, 64, 1), j) for i, j in zip(a, b)]
        return q, p

    for f in range(tiles):
        q, p = merge(starts, f)
        for v, a in enumerate(q + p):
            firsts[pl.ds(v * 8, 8), pl.ds(f * 128, 128)] = a
    firsts[STATES:256, :] = jnp.zeros((256 - STATES, runs), F32)
    firsts[0:STATES, :] = mm(phi[...], firsts[...])

    stores = []
    power_rows = []
    for f0 in range(0, tiles, 2):
        first = []
        for f in (f0, f0 + 1):
            q, p = merge(sin, f)
            q1, p1 = load_state(firsts.at[:, pl.ds(f * 128, 128)])
            q0, p0 = load_first(f)
            first += [a + b + c for a, b, c in zip(q + p, q1 + p1, q0 + p0)]

        def one(t, carry, f0=f0):
            w = own_w(t)
            o = obs_ref[t].astype(F32)
            preds = []
            for i in range(2):
                s = list(carry[i * both : (i + 1) * both])
                preds.append(leap(rows, s[:VREGS], s[VREGS:], w))
            new = [None] * (2 * both)
            square = [[rows.zero] * 4, [rows.zero] * 4]
            for v in range(both):
                gain = o * gain_rows[pl.ds(v * 8, 8), :]
                for i, (q, p) in enumerate(preds):
                    pred = (q + p)[v]
                    inn = mb[f0 + i, t, node(v), :] - pred
                    square[i][v % 4] = square[i][v % 4] + inn * inn
                    state = pred + gain * inn
                    mb[f0 + i, t, node(v), :] = state
                    new[i * both + v] = state
            out = [
                carry[2 * both + i] + o * ((square[i][0] + square[i][1]) + (square[i][2] + square[i][3]))
                for i in range(2)
            ]
            return (*new, *out)

        state = lax.fori_loop(0, here, one, (*first, rows.zero, rows.zero), unroll=2)
        for i in range(2):
            power_rows.append(jnp.sum(state[2 * both + i], axis=0, keepdims=True))
            f = f0 + i
            c = pltpu.make_async_copy(mb.at[f], out_hbm.at[:, :, pl.ds(f * 128, 128)], out_sem.at[f])
            c.start()
            stores.append(c)

    power = jnp.concatenate(power_rows + [jnp.zeros((8 - tiles, 128), F32)], axis=0)
    slot = 0
    for count, place, device in ((ring, r, ring_dev), (nx, x, x_dev), (nz, z, z_dev)):
        powers[slot + place] = power
        copies = []
        for k in range(1, count):
            ref = powers.at[slot + place]
            c = send(ref, ref, pw_s.at[slot + k], pw_r.at[slot + k], device(k))
            c.start()
            copies.append(c)
        for c in copies:
            c.wait()
        power = powers[slot]
        for k in range(1, count):
            power = power + powers[slot + k]
        slot += count
    total_steps = here * ring * nx * nz
    power_ref[...] = power[0:tiles] / F32(total_steps * STATES)
    for c in stores:
        c.wait()


def local(dims, measurements, observed, segment_ids, courant_table, filter_gains, initial_state):
    here, _, runs = measurements.shape
    nz, nx, ny = dims
    ring = ny * CORES
    tiles = runs // 128
    gains = filter_gains.reshape(1, STATES)
    vmem = pl.BlockSpec(memory_space=pltpu.VMEM)
    hbm = pl.BlockSpec(memory_space=pl.ANY)
    dma = pltpu.SemaphoreType.DMA
    packed = (SIDE, 128)
    filtered, power = pl.pallas_call(
        functools.partial(kernel, dims, runs, here),
        out_shape=(
            jax.ShapeDtypeStruct(measurements.shape, F32),
            jax.ShapeDtypeStruct((tiles, 128), F32),
        ),
        in_specs=[hbm] * 6,
        out_specs=(hbm, vmem),
        scratch_shapes=[
            pltpu.SMEM((here,), jnp.int32),
            pltpu.SMEM((here,), jnp.int32),
            pltpu.VMEM((SEGS, CABLES), F32),
            pltpu.VMEM((1, STATES), F32),
            dma((4,)),
            pltpu.VMEM((tiles, here, STATES, 128), F32),
            pltpu.VMEM((tiles, STATES, 128), F32),
            pltpu.VMEM((CABLES, SEGS, 128), F32),
            pltpu.VMEM((STATES, 256), F32),
            pltpu.VMEM((STATES, 128), F32),
            pltpu.VMEM((ring, *packed), F32),
            pltpu.VMEM((256, runs), F32),
            pltpu.VMEM((STATES, 128), F32),
            pltpu.VMEM((2, STATES, 128), F32),
            pltpu.VMEM((ring, 8, 128), jnp.int32),
            pltpu.SMEM((ring, 8, 128), jnp.int32),
            pltpu.VMEM((ring, *packed), F32),
            pltpu.VMEM((ring, *packed), F32),
            pltpu.VMEM((nx, STATES, 256), F32),
            pltpu.VMEM((nx + 1, 256, 256), F32),
            pltpu.VMEM((nx, *packed), F32),
            pltpu.VMEM((nx + 1, 256, 128), F32),
            pltpu.VMEM(packed, F32),
            pltpu.VMEM(packed, F32),
            pltpu.VMEM((256, 128), F32),
            pltpu.VMEM((ring, *packed), F32),
            pltpu.VMEM((ring, *packed), F32),
            pltpu.VMEM((ring + nx + nz, 8, 128), F32),
            dma((tiles,)),
            dma((tiles,)),
            dma((4,)),
            dma((ring,)),
            dma((ring,)),
            dma((ring,)),
            dma((ring,)),
            dma((nx,)),
            dma((nx,)),
            dma((nx,)),
            dma((nx,)),
            dma((nx,)),
            dma((nx,)),
            dma((1,)),
            dma((1,)),
            dma((ring,)),
            dma((ring,)),
            dma((ring,)),
            dma((ring,)),
            dma((1,)),
            dma((1,)),
            dma((ring + nx + nz,)),
            dma((ring + nx + nz,)),
        ],
        compiler_params=pltpu.CompilerParams(
            collective_id=0, has_side_effects=True, vmem_limit_bytes=48 << 20
        ),
    )(segment_ids, observed, courant_table, gains, measurements, initial_state)
    return filtered, power.reshape(runs)


def solution(mesh):
    dims = torus_of(mesh.size)
    in_specs = (P("tm", None, None), P("tm"), P("tm"), P(), P(), P())
    out_specs = (P("tm", None, None), P())
    return jax.shard_map(
        functools.partial(local, dims), mesh=mesh, in_specs=in_specs, out_specs=out_specs, check_vma=False
    )
```

```python
import functools

import jax
import jax.numpy as jnp
from jax import lax
from jax.experimental import pallas as pl
from jax.experimental.pallas import tpu as pltpu
from jax.sharding import PartitionSpec as P

CABLES = 4
HALF = 24
SIDE = CABLES * HALF
STATES = 2 * SIDE
SEGS = 32
PAYLOAD = 0.3
CORES = 2
MESH = pl.DeviceIdType.MESH
VREGS = SIDE // 8
F32 = jnp.float32


def torus_of(devices):
    return {128: (4, 4, 4), 16: (2, 2, 2)}[devices]


def lanes(tile):
    return pl.ds(pl.multiple_of(tile * 128, 128), 128)


class Rows:
    def __init__(self):
        row = lax.broadcasted_iota(jnp.int32, (8, 128), 0)
        self.first = row == 0
        self.last = row == 7
        self.pay = jnp.where(self.last, F32(PAYLOAD), F32(0.0))
        self.zero = jnp.zeros((8, 128), F32)
        self.low = lax.broadcasted_iota(jnp.int32, (8, 128), 1) < 64


def node(v):
    return pl.ds(HALF * (v // 3) + v % 3, 8, stride=3)


def leap(rows, q, p, w):
    total = (q[2] + q[5]) + (q[8] + q[11])
    wrap = [jnp.where(rows.first, rows.zero, pltpu.roll(q[3 * c + 2], 1, 0)) for c in range(CABLES)]
    new_p, u = [], []
    for v in range(VREGS):
        d = q[v] - (q[v - 1] if v % 3 else wrap[v // 3])
        if v % 3 == 2:
            d = d - rows.pay * (total - q[v])
        new_p.append(p[v] + w[v // 3] * d)
        u.append(w[v // 3] * new_p[v])
    wrap = [jnp.where(rows.last, rows.zero, pltpu.roll(u[3 * c], 7, 0)) for c in range(CABLES)]
    total = (u[2] + u[5]) + (u[8] + u[11])
    new_q = []
    for v in range(VREGS):
        e = u[v] - (u[v + 1] if v % 3 < 2 else wrap[v // 3])
        if v % 3 == 2:
            e = e - rows.pay * (total - u[v])
        new_q.append(q[v] - e)
    return new_q, new_p


def pack(rows, q, p, half):
    if half == 0:
        return [jnp.where(rows.low, a, pltpu.roll(b, 64, 1)) for a, b in zip(q, p)]
    return [jnp.where(rows.low, pltpu.roll(a, 64, 1), b) for a, b in zip(q, p)]


def kernel(
    dims, runs, steps,
    seg_hbm, obs_hbm, table_hbm, gains_hbm, m_hbm, x0_hbm,
    out_hbm, power_ref,
    seg_ref, obs_ref, table_ref, gains_ref, small_sem, mb, x0b, tab, phi, phi_out, starts, firsts, gain_rows, keep, params_v, params_s, bpack, bin_, maps, prefix, xin, sums, zin, zout,
    start, sout, sin, powers,
    m_sem, out_sem, loc_sem,
    par_s, par_r, up_s, up_r, mx_s, mx_r, mp_s, mp_r, x_s, x_r, z_s, z_r, dn_s, dn_r, st_s, st_r, ph_s, ph_r, pw_s, pw_r,
):
    nz, nx, ny = dims
    ring = ny * CORES
    here = steps
    tiles = runs // 128
    me = lax.axis_index("tm")
    r = lax.rem(me, ring)
    core = lax.rem(me, CORES)
    x = lax.rem(me // ring, nx)
    z = me // (ring * nx)
    base = me - r
    rows = Rows()

    def ring_dev(k):
        return base + lax.rem(r + k, ring)

    def x_dev(k):
        return (z * nx + lax.rem(x + k, nx)) * ring + r

    def z_dev(k):
        return (lax.rem(z + k, nz) * nx + x) * ring + r

    def send(src, dst, ssem, rsem, dev):
        return pltpu.make_async_remote_copy(
            src_ref=src, dst_ref=dst, send_sem=ssem, recv_sem=rsem, device_id=(dev,), device_id_type=MESH
        )

    smalls = []
    for i, (src, dst) in enumerate(
        ((seg_hbm, seg_ref), (obs_hbm, obs_ref), (table_hbm, table_ref), (gains_hbm, gains_ref))
    ):
        c = pltpu.make_async_copy(src, dst, small_sem.at[i])
        c.start()
        smalls.append(c)
    loads = []
    for f in range(tiles):
        c = pltpu.make_async_copy(m_hbm.at[:, :, pl.ds(f * 128, 128)], mb.at[f], m_sem.at[f])
        c.start()
        loads.append(c)

    barrier = pltpu.get_barrier_semaphore()
    for k in range(1, ring):
        pl.semaphore_signal(barrier, inc=1, device_id=(ring_dev(k),), device_id_type=MESH)
    for k in range(1, nx):
        pl.semaphore_signal(barrier, inc=1, device_id=(x_dev(k),), device_id_type=MESH)
    for k in range(1, nz):
        pl.semaphore_signal(barrier, inc=1, device_id=(z_dev(k),), device_id_type=MESH)

    @pl.when(me == 0)
    def _():
        copies = []
        for f in range(tiles):
            c = pltpu.make_async_copy(x0_hbm.at[:, pl.ds(f * 128, 128)], x0b.at[f], loc_sem.at[0])
            c.start()
            copies.append(c)
        for c in copies:
            c.wait()

    @pl.when(me > 0)
    def _():
        x0b[...] = jnp.zeros_like(x0b)

    for c in smalls:
        c.wait()

    row_i = lax.broadcasted_iota(jnp.int32, (8, 128), 0)
    lane_i = lax.broadcasted_iota(jnp.int32, (8, 128), 1)
    tile = jnp.zeros((8, 128), jnp.int32)
    for t in range(here):
        tile = jnp.where((row_i == 0) & (lane_i == t), seg_ref[t], tile)
        tile = jnp.where((row_i == 1) & (lane_i == t), obs_ref[t], tile)
    params_v[r] = tile

    gain_lanes = [
        gains_ref[0:1, 0:128],
        jnp.concatenate([gains_ref[0:1, 128:STATES], jnp.zeros((1, 256 - STATES), F32)], axis=1),
    ]
    for v in range(STATES // 8):
        spread = jnp.zeros((8, 1), F32)
        for part in range(2):
            g = jnp.broadcast_to(gain_lanes[part], (8, 128))
            spread = spread + jnp.sum(
                jnp.where(lane_i + part * 128 == row_i * 3 + (HALF * (v // 3) + v % 3), g, F32(0.0)), axis=1, keepdims=True
            )
        g = jnp.broadcast_to(spread, (8, 128))
        gain_rows[pl.ds(v * 8, 8), :] = g
        keep[0, pl.ds(v * 8, 8), :] = jnp.ones((8, 128), F32)
        keep[1, pl.ds(v * 8, 8), :] = 1.0 - g

    seg_row = lax.broadcasted_iota(jnp.int32, (8, SEGS), 0)
    seg_lane = lax.broadcasted_iota(jnp.int32, (8, SEGS), 1)
    for c in range(CABLES):
        for s in range(SEGS // 8):
            g = jnp.broadcast_to(table_ref[c : c + 1, :], (8, SEGS))
            g = jnp.where(seg_lane == seg_row + s * 8, g, F32(0.0))
            tab[c, s * 8 : s * 8 + 8, :] = jnp.broadcast_to(jnp.sum(g, axis=1, keepdims=True), (8, 128))

    def spread_w(s):
        return [jnp.broadcast_to(tab[c, pl.ds(s, 1), :], (8, 128)) for c in range(CABLES)]

    pl.semaphore_wait(barrier, (ring - 1) + (nx - 1) + (nz - 1))

    par = []
    for k in range(1, ring):
        c = send(params_v.at[r], params_v.at[r], par_s.at[k], par_r.at[k], ring_dev(k))
        c.start()
        par.append(c)

    def load_state(ref_q):
        return (
            [ref_q[pl.ds(v * 8, 8), :] for v in range(VREGS)],
            [ref_q[pl.ds(SIDE + v * 8, 8), :] for v in range(VREGS)],
        )

    def load_first(f):
        return (
            [x0b[f, node(v), :] for v in range(VREGS)],
            [x0b[f, node(VREGS + v), :] for v in range(VREGS)],
        )

    def own_w(t):
        return spread_w(seg_ref[t])

    ups = {}
    both = 2 * VREGS
    for f0 in range(0, tiles, 2):
        loads[f0].wait()
        loads[f0 + 1].wait()

        def one(t, carry, f0=f0):
            w = own_w(t)
            o = obs_ref[t].astype(F32)
            preds = []
            for i in range(2):
                s = list(carry[i * both : (i + 1) * both])
                preds.append(leap(rows, s[:VREGS], s[VREGS:], w))
            new = [None] * (2 * both)
            for v in range(both):
                gain = o * gain_rows[pl.ds(v * 8, 8), :]
                for i, (q, p) in enumerate(preds):
                    pred = (q + p)[v]
                    new[i * both + v] = pred + gain * (mb[f0 + i, t, node(v), :] - pred)
            return tuple(new)

        first = [load_first(f0), load_first(f0 + 1)]
        state = lax.fori_loop(0, here, one, tuple(a for q, p in first for a in q + p), unroll=2)
        for i in range(2):
            s = list(state[i * both : (i + 1) * both])
            for half in range(2):
                packed = pack(rows, s[:VREGS], s[VREGS:], half)
                for v in range(VREGS):
                    bpack[2 * (f0 + i) + half, pl.ds(v * 8, 8), :] = packed[v]
    for k in range(1, ring):
        peer = lax.rem(r + k, ring)
        c = send(bpack.at[peer], bin_.at[r], up_s.at[k], up_r.at[k], ring_dev(k))
        c.start()
        ups[k] = c
    own = pltpu.make_async_copy(bpack.at[r], bin_.at[r], loc_sem.at[1])
    own.start()

    for c in par:
        c.wait()
    ints = pltpu.make_async_copy(params_v, params_s, loc_sem.at[2])
    ints.start()
    ints.wait()

    def step_free(carry, j, t):
        q, p = list(carry[:VREGS]), list(carry[VREGS:])
        s = params_s[j, 0, t]
        o = params_s[j, 1, t]
        q, p = leap(rows, q, p, spread_w(s))
        return tuple(a * keep[o, pl.ds(v * 8, 8), :] for v, a in enumerate(q + p))

    def block_free(carry, j):
        return lax.fori_loop(0, here, lambda t, s: step_free(s, j, t), carry, unroll=4)

    col = lane_i + core * 128
    state = tuple(jnp.where(col == row_i + v * 8, F32(1.0), F32(0.0)) for v in range(2 * VREGS))
    mate = me + 1 - 2 * core
    mate_r = r + 1 - 2 * core

    def climb(j, carry):
        @pl.when(j == r)
        def _():
            for v, a in enumerate(carry):
                phi[pl.ds(v * 8, 8), lanes(core)] = a

        @pl.when(j == mate_r)
        def _():
            for v, a in enumerate(carry):
                phi_out[pl.ds(v * 8, 8), :] = a

        return block_free(carry, j)

    state = lax.fori_loop(0, ring, climb, state)
    for v in range(2 * VREGS):
        maps[x, pl.ds(v * 8, 8), lanes(core)] = state[v]
    mine = maps.at[x, :, lanes(core)]
    mxs = []
    for k in range(1, nx):
        c = send(mine, mine, mx_s.at[k], mx_r.at[k], x_dev(k))
        c.start()
        mxs.append(c)
    mps = [send(mine, mine, mp_s.at[0], mp_r.at[0], mate)]
    mps[0].start()

    phic = send(phi_out, phi.at[:, lanes(core)], ph_s.at[0], ph_r.at[0], mate)
    phic.start()

    for k in range(1, ring):
        ups[k].wait()
    own.wait()

    def unpack(ref):
        a = [ref[pl.ds(v * 8, 8), :] for v in range(VREGS)]
        return a, [pltpu.roll(v, 64, 1) for v in a]

    def put(carry, j):
        for v, a in enumerate(pack(rows, list(carry[:VREGS]), list(carry[VREGS:]), 0)):
            sout[j, pl.ds(v * 8, 8), :] = a

    for v in range(VREGS):
        sout[0, pl.ds(v * 8, 8), :] = rows.zero
    q, p = unpack(bin_.at[0])

    def rise(j, carry):
        put(carry, j)
        carry = block_free(carry, j)
        q, p = unpack(bin_.at[j])
        return tuple(a + b for a, b in zip(carry, q + p))

    state = lax.fori_loop(1, ring, rise, tuple(q + p))
    packed = pack(rows, list(state[:VREGS]), list(state[VREGS:]), 0)
    for v in range(VREGS):
        xin[x, pl.ds(v * 8, 8), :] = packed[v]
    xs = []
    for k in range(1, nx):
        c = send(xin.at[x], xin.at[x], x_s.at[k], x_r.at[k], x_dev(k))
        c.start()
        xs.append(c)

    downs = []
    for k in range(1, ring):
        peer = lax.rem(r + k, ring)
        c = send(sout.at[peer], sin.at[r], dn_s.at[k], dn_r.at[k], ring_dev(k))
        c.start()
        downs.append(c)
    own_down = pltpu.make_async_copy(sout.at[r], sin.at[r], loc_sem.at[3])
    own_down.start()

    for k in range(1, nx):
        mxs[k - 1].wait()
        there = lax.rem(x + nx - k, nx)
        src = maps.at[there, :, lanes(core)]
        c = send(src, src, mp_s.at[k], mp_r.at[k], mate)
        c.start()
        mps.append(c)
    for c in mps:
        c.wait()

    def mm(a, b):
        return jnp.dot(a, b, precision=lax.Precision.HIGHEST, preferred_element_type=F32)

    pad = jnp.zeros((256 - STATES, 128), F32)

    row2 = lax.broadcasted_iota(jnp.int32, (256, 256), 0)
    col2 = lax.broadcasted_iota(jnp.int32, (256, 256), 1)
    prefix[0] = jnp.where(row2 == col2, F32(1.0), F32(0.0))
    for i in range(nx):
        prefix[i + 1, 0:STATES, :] = mm(maps[i], prefix[i])
        prefix[i + 1, STATES:256, :] = jnp.zeros((256 - STATES, 256), F32)

    for c in xs:
        c.wait()
    sums[0] = jnp.zeros((256, 128), F32)
    for i in range(nx):
        q, p = unpack(xin.at[i])
        b = jnp.concatenate(q + p, axis=0)
        if i:
            b = b + mm(maps[i], sums[i])
        sums[i + 1, 0:STATES, :] = b
        sums[i + 1, STATES:256, :] = pad

    zcopy = send(zout, zin, z_s.at[0], z_r.at[0], z_dev(1))
    start[...] = jnp.zeros_like(start)

    @pl.when(z > 0)
    def _():
        zcopy.wait_recv()
        q, p = unpack(zin)
        for v, a in enumerate(q + p):
            start[pl.ds(v * 8, 8), :] = a

    @pl.when(z < nz - 1)
    def _():
        s = mm(prefix[nx, 0:STATES, :], start[...]) + sums[nx, 0:STATES, :]
        q = [s[v * 8 : v * 8 + 8] for v in range(VREGS)]
        p = [s[SIDE + v * 8 : SIDE + v * 8 + 8] for v in range(VREGS)]
        for v, a in enumerate(pack(rows, q, p, 0)):
            zout[pl.ds(v * 8, 8), :] = a
        zcopy.start()
        zcopy.wait_send()

    start[0:STATES, :] = mm(prefix[x, 0:STATES, :], start[...]) + sums[x, 0:STATES, :]

    q, p = load_state(start)
    for v, a in enumerate(pack(rows, q, p, 0)):
        starts[r, pl.ds(v * 8, 8), :] = a
    sts = []
    for k in range(1, ring):
        c = send(starts.at[r], starts.at[r], st_s.at[k], st_r.at[k], ring_dev(k))
        c.start()
        sts.append(c)
    phic.wait()
    for c in downs:
        c.wait()
    own_down.wait()
    for c in sts:
        c.wait()

    def merge(ref, f):
        a = [ref[2 * f, pl.ds(v * 8, 8), :] for v in range(VREGS)]
        b = [ref[2 * f + 1, pl.ds(v * 8, 8), :] for v in range(VREGS)]
        q = [jnp.where(rows.low, i, pltpu.roll(j, 64, 1)) for i, j in zip(a, b)]
        p = [jnp.where(rows.low, pltpu.roll(i, 64, 1), j) for i, j in zip(a, b)]
        return q, p

    for f in range(tiles):
        q, p = merge(starts, f)
        for v, a in enumerate(q + p):
            firsts[pl.ds(v * 8, 8), pl.ds(f * 128, 128)] = a
    firsts[STATES:256, :] = jnp.zeros((256 - STATES, runs), F32)
    firsts[0:STATES, :] = mm(phi[...], firsts[...])

    stores = []
    power_rows = []
    for f0 in range(0, tiles, 2):
        first = []
        for f in (f0, f0 + 1):
            q, p = merge(sin, f)
            q1, p1 = load_state(firsts.at[:, pl.ds(f * 128, 128)])
            q0, p0 = load_first(f)
            first += [a + b + c for a, b, c in zip(q + p, q1 + p1, q0 + p0)]

        def one(t, carry, f0=f0):
            w = own_w(t)
            o = obs_ref[t].astype(F32)
            preds = []
            for i in range(2):
                s = list(carry[i * both : (i + 1) * both])
                preds.append(leap(rows, s[:VREGS], s[VREGS:], w))
            new = [None] * (2 * both)
            square = [[rows.zero] * 4, [rows.zero] * 4]
            for v in range(both):
                gain = o * gain_rows[pl.ds(v * 8, 8), :]
                for i, (q, p) in enumerate(preds):
                    pred = (q + p)[v]
                    inn = mb[f0 + i, t, node(v), :] - pred
                    square[i][v % 4] = square[i][v % 4] + inn * inn
                    state = pred + gain * inn
                    mb[f0 + i, t, node(v), :] = state
                    new[i * both + v] = state
            out = [
                carry[2 * both + i] + o * ((square[i][0] + square[i][1]) + (square[i][2] + square[i][3]))
                for i in range(2)
            ]
            return (*new, *out)

        state = lax.fori_loop(0, here, one, (*first, rows.zero, rows.zero), unroll=2)
        for i in range(2):
            power_rows.append(jnp.sum(state[2 * both + i], axis=0, keepdims=True))
            f = f0 + i
            c = pltpu.make_async_copy(mb.at[f], out_hbm.at[:, :, pl.ds(f * 128, 128)], out_sem.at[f])
            c.start()
            stores.append(c)

    power = jnp.concatenate(power_rows + [jnp.zeros((8 - tiles, 128), F32)], axis=0)
    slot = 0
    for count, place, device in ((ring, r, ring_dev), (nx, x, x_dev), (nz, z, z_dev)):
        powers[slot + place] = power
        copies = []
        for k in range(1, count):
            ref = powers.at[slot + place]
            c = send(ref, ref, pw_s.at[slot + k], pw_r.at[slot + k], device(k))
            c.start()
            copies.append(c)
        for c in copies:
            c.wait()
        power = powers[slot]
        for k in range(1, count):
            power = power + powers[slot + k]
        slot += count
    total_steps = here * ring * nx * nz
    power = power / F32(total_steps * STATES)
    for f in range(tiles):
        power_ref[0:1, f * 128 : f * 128 + 128] = power[f : f + 1]
    for c in stores:
        c.wait()


def local(dims, measurements, observed, segment_ids, courant_table, filter_gains, initial_state):
    here, _, runs = measurements.shape
    nz, nx, ny = dims
    ring = ny * CORES
    tiles = runs // 128
    gains = filter_gains.reshape(1, STATES)
    vmem = pl.BlockSpec(memory_space=pltpu.VMEM)
    hbm = pl.BlockSpec(memory_space=pltpu.HBM)
    dma = pltpu.SemaphoreType.DMA
    packed = (SIDE, 128)
    filtered, power = pl.pallas_call(
        functools.partial(kernel, dims, runs, here),
        out_shape=(
            jax.ShapeDtypeStruct(measurements.shape, F32),
            jax.ShapeDtypeStruct((1, runs), F32),
        ),
        in_specs=[hbm] * 6,
        out_specs=(hbm, vmem),
        scratch_shapes=[
            pltpu.SMEM((here,), jnp.int32),
            pltpu.SMEM((here,), jnp.int32),
            pltpu.VMEM((CABLES, SEGS), F32),
            pltpu.VMEM((1, STATES), F32),
            dma((4,)),
            pltpu.VMEM((tiles, here, STATES, 128), F32),
            pltpu.VMEM((tiles, STATES, 128), F32),
            pltpu.VMEM((CABLES, SEGS, 128), F32),
            pltpu.VMEM((STATES, 256), F32),
            pltpu.VMEM((STATES, 128), F32),
            pltpu.VMEM((ring, *packed), F32),
            pltpu.VMEM((256, runs), F32),
            pltpu.VMEM((STATES, 128), F32),
            pltpu.VMEM((2, STATES, 128), F32),
            pltpu.VMEM((ring, 8, 128), jnp.int32),
            pltpu.SMEM((ring, 8, 128), jnp.int32),
            pltpu.VMEM((ring, *packed), F32),
            pltpu.VMEM((ring, *packed), F32),
            pltpu.VMEM((nx, STATES, 256), F32),
            pltpu.VMEM((nx + 1, 256, 256), F32),
            pltpu.VMEM((nx, *packed), F32),
            pltpu.VMEM((nx + 1, 256, 128), F32),
            pltpu.VMEM(packed, F32),
            pltpu.VMEM(packed, F32),
            pltpu.VMEM((256, 128), F32),
            pltpu.VMEM((ring, *packed), F32),
            pltpu.VMEM((ring, *packed), F32),
            pltpu.VMEM((ring + nx + nz, 8, 128), F32),
            dma((tiles,)),
            dma((tiles,)),
            dma((4,)),
            dma((ring,)),
            dma((ring,)),
            dma((ring,)),
            dma((ring,)),
            dma((nx,)),
            dma((nx,)),
            dma((nx,)),
            dma((nx,)),
            dma((nx,)),
            dma((nx,)),
            dma((1,)),
            dma((1,)),
            dma((ring,)),
            dma((ring,)),
            dma((ring,)),
            dma((ring,)),
            dma((1,)),
            dma((1,)),
            dma((ring + nx + nz,)),
            dma((ring + nx + nz,)),
        ],
        compiler_params=pltpu.CompilerParams(
            collective_id=0, has_side_effects=True, vmem_limit_bytes=48 << 20
        ),
    )(segment_ids, observed, courant_table.T, gains, measurements, initial_state)
    return filtered, power.reshape(runs)


def solution(mesh):
    dims = torus_of(mesh.size)
    in_specs = (P("tm", None, None), P("tm"), P("tm"), P(), P(), P())
    out_specs = (P("tm", None, None), P())
    return jax.shard_map(
        functools.partial(local, dims), mesh=mesh, in_specs=in_specs, out_specs=out_specs, check_vma=False
    )
```
